32 devices in a mesh: section: 4 (over z), seq: 8 (over y, x, core).
Axes of the slice: x: 2, y: 2, z: 4, core: 2. Of those that a mesh axis runs over, the one named last changes fastest.
Arguments:
- queries: bfloat16 [4, 2, 1024, 4096], P('section', None, 'seq'), may hold values from -80 to 80
- keys_new: bfloat16 [4, 2, 1024, 1024], P('section', None, 'seq'), may hold values from -4 to 4
- values_new: bfloat16 [4, 2, 1024, 1024], P('section', None, 'seq'), may hold values from -6 to 6
- key_cache: bfloat16 [4, 32, 4096, 128], P('section', 'seq'), may hold values from -6 to 6
- value_cache: bfloat16 [4, 32, 4096, 128], P('section', 'seq'), may hold values from -6 to 6
- block_lists: int32 [4, 32, 2, 16, 32], P('section', 'seq'), may hold values from 0 to 63, as said below
- block_counts: int32 [4, 32, 2, 16], P('section', 'seq'), may hold values from 1 to 32
- visible_blocks: int32 [2], replicated, may hold values from 32 to 64
Outputs:
- handed: bfloat16 [4, 2, 1024, 4096], P('section', None, 'seq')
The draws below stay inside these ranges and needn't reach their ends.
Inputs may be any that keep to these rules, and one draw needn't show every extreme that they name: `block_lists`: each list holds 32 different block numbers.
All inputs are finite; a program needn't handle non-finite values.
Results may differ from the reference program's by a relative error of at most 0.003.
Values may be sent and summed in bfloat16 or wider, within the bound.
A program may use at most 192 MiB of HBM per device.

```python
from functools import partial
import jax
import jax.numpy as jnp
from jax import lax

HEADS = 32
KVH = 8
DH = 128
SPAN = 1024
SPANS = 2
BLK = 64
CTX = 4096
NSEL = 32
LAYERS = 4
QBLOCKS = 16
CACHE_BLOCKS = 64


def joint_draw(key):
    key_query, key_keys = jax.random.split(jax.random.fold_in(key, 7))
    group_size = HEADS // KVH
    keys_drawn = jnp.clip(jax.random.normal(key_keys, (LAYERS, SPANS, SPAN, KVH, 1, DH), jnp.float32), -4.0, 4.0)
    query_drawn = jnp.clip(2.5 * jax.random.normal(key_query, (LAYERS, SPANS, SPAN, KVH, group_size, DH), jnp.float32), -12.0, 12.0)
    query_out = query_drawn.reshape(LAYERS, SPANS, SPAN, HEADS * DH)
    keys_out = keys_drawn.reshape(LAYERS, SPANS, SPAN, KVH * DH)
    return (query_out, keys_out)


def draw_queries(key, part):
    return joint_draw(key)[0].astype(jnp.bfloat16)


def draw_keys_new(key, part):
    return joint_draw(key)[1].astype(jnp.bfloat16)


def pick_permutation(sub_key):
    return jax.random.permutation(sub_key, CACHE_BLOCKS)


def draw_block_lists(key, part):
    list_total = LAYERS * HEADS * SPANS * QBLOCKS
    sub_keys = jax.random.split(jax.random.fold_in(key, 21), list_total)
    chosen = jax.vmap(pick_permutation)(sub_keys)[:, :NSEL]
    return chosen.reshape(LAYERS, HEADS, SPANS, QBLOCKS, NSEL).astype(jnp.int32)


def draw_block_counts(key, part):
    key_cap, key_raw, key_spot = jax.random.split(jax.random.fold_in(key, 33), 3)
    head_cap = jax.random.randint(key_cap, (LAYERS, HEADS, 1, 1), NSEL // 4, NSEL + 1)
    raw_value = jax.random.randint(key_raw, (LAYERS, HEADS, SPANS, QBLOCKS), 0, 1 << 20)
    counted = 1 + raw_value % head_cap
    list_total = LAYERS * HEADS * SPANS * QBLOCKS
    spot_index = jax.random.randint(key_spot, (), 0, list_total)
    flat_counts = jnp.where(jnp.arange(list_total) == spot_index, NSEL, counted.reshape(list_total))
    return flat_counts.reshape(LAYERS, HEADS, SPANS, QBLOCKS).astype(jnp.int32)


def levels(rng, extent, shards, smallest, top_value):
    gain, own = 1.0, jax.random.fold_in(rng, 6)
    for dim, blocks in shards:
        heights = jnp.exp(jax.random.uniform(jax.random.fold_in(own, dim), (blocks,), jnp.float32, smallest / len(shards), top_value / len(shards)))
        gain = gain * jnp.repeat(heights, extent[dim] // blocks).reshape([-1 if axis == dim else 1 for axis in range(len(extent))])
    return gain


def bell_draw(stream_key, dims, width, limit, cuts=(), kind=jnp.bfloat16):
    gain = levels(stream_key, dims, cuts, -0.22, 0.18) if cuts else 1.0
    result = jax.random.normal(stream_key, dims, jnp.float32) * width * gain
    return jnp.minimum(jnp.maximum(result, -limit), limit).astype(kind)


def setup_inputs(seed: int = 0) -> dict:
    splits = jax.random.split(jax.random.key(seed), 9)
    return {
        "queries": draw_queries(jax.random.fold_in(splits[8], 71), 0),
        "keys_new": draw_keys_new(jax.random.fold_in(splits[8], 71), 0),
        "values_new": bell_draw(splits[2], (LAYERS, SPANS, SPAN, KVH * DH), 1.0, 6.0, ((0, 4), (2, 8))),
        "key_cache": bell_draw(splits[3], (LAYERS, HEADS, CTX, DH), 1.0, 6.0, ((0, 4), (1, 8))),
        "value_cache": bell_draw(splits[4], (LAYERS, HEADS, CTX, DH), 1.0, 6.0, ((0, 4), (1, 8))),
        "block_lists": draw_block_lists(jax.random.fold_in(splits[8], 71), 0),
        "block_counts": draw_block_counts(jax.random.fold_in(splits[8], 71), 0),
        "visible_blocks": jax.random.randint(splits[7], (SPANS,), CACHE_BLOCKS // 2, CACHE_BLOCKS + 1).astype(jnp.int32),
    }


def head_attention(visible_blocks, items):
    query_head, key_head, value_head, cache_keys, cache_values, lists_head, counts_head = items
    score_scale = 1.0 / (DH ** 0.5)
    results = []
    for span_index in range(SPANS):
        query_float = query_head[span_index].astype(jnp.float32)
        own_scores = jnp.einsum("rd,kd->rk", query_float, key_head[span_index].astype(jnp.float32), precision=lax.Precision.HIGHEST) * score_scale
        causal = jnp.arange(SPAN)[:, None] >= jnp.arange(SPAN)[None, :]
        own_scores = jnp.where(causal, own_scores, -jnp.inf)
        chosen = lists_head[span_index]
        key_blocks = cache_keys[chosen].astype(jnp.float32)
        cache_scores = jnp.einsum("qbd,qjtd->qbjt", query_float.reshape(QBLOCKS, BLK, DH), key_blocks, precision=lax.Precision.HIGHEST) * score_scale
        usable = (jnp.arange(NSEL)[None, :] < counts_head[span_index][:, None]) & (chosen < visible_blocks[span_index])
        cache_scores = jnp.where(usable[:, None, :, None], cache_scores, -jnp.inf).reshape(QBLOCKS, BLK, NSEL * BLK)
        every_score = jnp.concatenate([cache_scores, own_scores.reshape(QBLOCKS, BLK, SPAN)], axis=2)
        row_max = jnp.max(every_score, axis=2, keepdims=True)
        weights = jnp.exp(every_score - row_max)
        row_sum = jnp.sum(weights, axis=2)
        weights_b = weights.astype(jnp.bfloat16).astype(jnp.float32)
        value_blocks = cache_values[chosen].astype(jnp.float32).reshape(QBLOCKS, NSEL * BLK, DH)
        mixed = jnp.einsum("qbk,qkd->qbd", weights_b[:, :, :NSEL * BLK], value_blocks, precision=lax.Precision.HIGHEST)
        mixed = mixed + jnp.einsum("qbk,kd->qbd", weights_b[:, :, NSEL * BLK:], value_head[span_index].astype(jnp.float32), precision=lax.Precision.HIGHEST)
        results.append((mixed / row_sum[:, :, None]).astype(jnp.bfloat16).reshape(SPAN, DH))
    return jnp.stack(results)


def reference(queries, keys_new, values_new, key_cache, value_cache, block_lists, block_counts, visible_blocks):
    group_size = HEADS // KVH
    layers = queries.shape[0]
    query_heads = queries.reshape(layers, SPANS, SPAN, HEADS, DH).transpose(0, 3, 1, 2, 4).reshape(layers * HEADS, SPANS, SPAN, DH)
    key_heads = jnp.repeat(keys_new.reshape(layers, SPANS, SPAN, KVH, DH), group_size, axis=3)
    key_heads = key_heads.transpose(0, 3, 1, 2, 4).reshape(layers * HEADS, SPANS, SPAN, DH)
    value_heads = jnp.repeat(values_new.reshape(layers, SPANS, SPAN, KVH, DH), group_size, axis=3)
    value_heads = value_heads.transpose(0, 3, 1, 2, 4).reshape(layers * HEADS, SPANS, SPAN, DH)
    cache_keys = key_cache.reshape(layers * HEADS, CACHE_BLOCKS, BLK, DH)
    cache_values = value_cache.reshape(layers * HEADS, CACHE_BLOCKS, BLK, DH)
    lists_all = block_lists.reshape(layers * HEADS, SPANS, QBLOCKS, NSEL)
    counts_all = block_counts.reshape(layers * HEADS, SPANS, QBLOCKS)
    outputs = lax.map(partial(head_attention, visible_blocks), (query_heads, key_heads, value_heads, cache_keys, cache_values, lists_all, counts_all))
    attended = outputs.reshape(layers, HEADS, SPANS, SPAN, DH).transpose(0, 2, 3, 1, 4).reshape(layers, SPANS, SPAN, HEADS * DH)
    return jnp.roll(attended, 1, axis=0)
```

```python
import functools
import math

import jax
import jax.numpy as jnp
from jax import lax
from jax.experimental import pallas as pl
from jax.experimental.pallas import tpu as pltpu
from jax.sharding import PartitionSpec as P

HEADS = 32
KVH = 8
DH = 128
BLK = 64
GROUP = HEADS // KVH
ROW_TILE = 256
CHUNK = 4
TASKS = 2


def mesh_copy(src, dst, send_sem, recv_sem, section, seq):
    return pltpu.make_async_remote_copy(
        src_ref=src,
        dst_ref=dst,
        send_sem=send_sem,
        recv_sem=recv_sem,
        device_id=(section, seq),
        device_id_type=pl.DeviceIdType.MESH,
    )


def scores_of(query, keys):
    return lax.dot_general(
        query, keys, (((1,), (1,)), ((), ())), preferred_element_type=jnp.float32
    )


def fused(
    n,
    sections,
    lists,
    biases,
    queries,
    keys_new,
    values_new,
    key_cache,
    value_cache,
    out,
    qbuf,
    kbuf,
    vbuf,
    ckeys,
    cvalues,
    att,
    own_max,
    own_sum,
    own_out,
    in_send,
    in_recv,
    in_local,
    cache_sem,
    out_send,
    out_recv,
):
    spans, heads, span_len = qbuf.shape[0], qbuf.shape[1], qbuf.shape[2]
    kv_dev = kbuf.shape[1]
    rows = queries.shape[2]
    slots = lists.shape[1]
    query_blocks = span_len // BLK
    items = 2 * kv_dev + heads
    weight_scale = math.log2(math.e) / math.sqrt(DH)
    section = lax.axis_index("section")
    me = lax.axis_index("seq")
    above = lax.rem(section + 1, sections)
    below = lax.rem(section + sections - 1, sections)

    for head in range(heads):
        pltpu.make_async_copy(key_cache.at[0, head], ckeys.at[head], cache_sem.at[0, head]).start()
        pltpu.make_async_copy(
            value_cache.at[0, head], cvalues.at[head], cache_sem.at[1, head]
        ).start()

    def source(span, item, seq):
        if isinstance(item, int) and item < 2 * kv_dev:
            array = keys_new if item < kv_dev else values_new
            column = lax.div(seq * heads, GROUP) * DH + (item % kv_dev) * DH
        else:
            array = queries
            column = (seq * heads + item - 2 * kv_dev) * DH
        return array.at[0, span, :, pl.ds(pl.multiple_of(column, DH), DH)]

    def landing(span, item, seq):
        where = pl.ds(pl.multiple_of(seq * rows, rows), rows)
        if isinstance(item, int) and item < kv_dev:
            return kbuf.at[span, item, where, :]
        if isinstance(item, int) and item < 2 * kv_dev:
            return vbuf.at[span, item - kv_dev, where, :]
        return qbuf.at[span, item - 2 * kv_dev, where, :]

    def own_copy(span, item):
        return pltpu.make_async_copy(
            source(span, item, me), landing(span, item, me), in_local.at[span, item]
        )

    for span in range(spans):
        for item in range(items):
            own_copy(span, item).start()

    barrier = pltpu.get_barrier_semaphore()

    def greet(k, carry):
        @pl.when(k > 0)
        def _():
            pl.semaphore_signal(
                barrier,
                inc=1,
                device_id=(section, lax.rem(me + k, n)),
                device_id_type=pl.DeviceIdType.MESH,
            )

        for there in (above, below):
            pl.semaphore_signal(
                barrier,
                inc=1,
                device_id=(there, lax.rem(me + k, n)),
                device_id_type=pl.DeviceIdType.MESH,
            )
        return carry

    lax.fori_loop(0, n, greet, 0)
    pl.semaphore_wait(barrier, 3 * n - 1)

    def in_copy(span, item, k, seq_to, seq_from):
        return mesh_copy(
            source(span, item, seq_to),
            landing(span, item, seq_from),
            in_send.at[span, item, k],
            in_recv.at[span, item, k],
            section,
            seq_to,
        )

    for span in range(spans):
        for item in range(items):

            def send_in(k, carry):
                in_copy(span, item, k, lax.rem(me + k, n), me).start()
                return carry

            lax.fori_loop(1, n, send_in, 0)

    def await_in(span, item):
        own_copy(span, item).wait()

        def one(k, carry):
            in_copy(
                span, item, k, lax.rem(me + k, n), lax.rem(me + n - k, n)
            ).wait_recv()
            return carry

        lax.fori_loop(1, n, one, 0)

    def out_copy(span, head, k, seq_to, seq_from):
        column = pl.multiple_of((seq_from * heads + head) * DH, DH)
        return mesh_copy(
            att.at[span, head, pl.ds(pl.multiple_of(seq_to * rows, rows), rows), :],
            out.at[0, span, :, pl.ds(column, DH)],
            out_send.at[span, head, k],
            out_recv.at[span, head, k],
            above,
            seq_to,
        )

    row_at = lax.broadcasted_iota(jnp.int32, (ROW_TILE, ROW_TILE), 0)
    key_at = lax.broadcasted_iota(jnp.int32, (ROW_TILE, ROW_TILE), 1)

    def weigh(scores, top):
        return jnp.exp2((scores - top) * weight_scale)

    def own_part(span, head, kv, tile):
        start = tile * ROW_TILE
        query = qbuf[span, head, start : start + ROW_TILE, :]
        parts = []
        for piece in range(tile + 1):
            keys = kbuf[span, kv, piece * ROW_TILE : (piece + 1) * ROW_TILE, :]
            scores = scores_of(query, keys)
            if piece == tile:
                scores = jnp.where(row_at >= key_at, scores, -jnp.inf)
            parts.append(scores)
        top = jnp.max(functools.reduce(jnp.maximum, parts), axis=1, keepdims=True)
        summed, mixed = None, None
        for piece, scores in enumerate(parts):
            weights = weigh(scores, top)
            values = vbuf[span, kv, piece * ROW_TILE : (piece + 1) * ROW_TILE, :]
            product = jnp.dot(
                weights.astype(jnp.bfloat16), values, preferred_element_type=jnp.float32
            )
            summed = weights if summed is None else summed + weights
            mixed = product if mixed is None else mixed + product
        total = jnp.sum(summed, axis=1, keepdims=True)
        own_max[start : start + ROW_TILE, :] = jnp.broadcast_to(top, (ROW_TILE, DH))
        own_sum[start : start + ROW_TILE, :] = jnp.broadcast_to(total, (ROW_TILE, DH))
        own_out[start : start + ROW_TILE, :] = mixed

    def cache_part(span, head, block):
        listed = (head * spans + span) * query_blocks + block
        at = pl.ds(pl.multiple_of(block * BLK, BLK), BLK)
        query = qbuf[span, head, at, :]
        chosen = [lists[listed, i] for i in range(slots)]
        bias = biases[listed]
        parts = []
        for first in range(0, slots, CHUNK):
            keys = jnp.concatenate(
                [
                    ckeys[head, chosen[i]]
                    for i in range(first, first + CHUNK)
                ],
                axis=0,
            )
            scores = scores_of(query, keys)
            parts.append(scores + bias[first // CHUNK : first // CHUNK + 1, :])
        before = own_max[at, :][:, :1]
        top = jnp.max(functools.reduce(jnp.maximum, parts), axis=1, keepdims=True)
        top = jnp.maximum(top, before)
        summed, mixed = None, None
        for step, scores in enumerate(parts):
            weights = weigh(scores, top)
            values = jnp.concatenate(
                [
                    cvalues[head, chosen[i]]
                    for i in range(step * CHUNK, (step + 1) * CHUNK)
                ],
                axis=0,
            )
            product = jnp.dot(
                weights.astype(jnp.bfloat16), values, preferred_element_type=jnp.float32
            )
            summed = weights if summed is None else summed + weights
            mixed = product if mixed is None else mixed + product
        fade = weigh(before, top)
        total = jnp.sum(summed, axis=1, keepdims=True) + own_sum[at, :][:, :1] * fade
        return ((mixed + own_out[at, :] * fade) / total).astype(jnp.bfloat16)

    for head in range(heads):
        pltpu.make_async_copy(key_cache.at[0, head], ckeys.at[head], cache_sem.at[0, head]).wait()
        pltpu.make_async_copy(
            value_cache.at[0, head], cvalues.at[head], cache_sem.at[1, head]
        ).wait()

    for span in range(spans):
        for item in range(2 * kv_dev):
            await_in(span, item)

        def one_head(head, carry):
            kv = lax.div(head, GROUP)
            await_in(span, 2 * kv_dev + head)
            for tile in range(span_len // ROW_TILE):
                own_part(span, head, kv, tile)

            def tasks(step, inner):
                done = [cache_part(span, head, step * TASKS + t) for t in range(TASKS)]
                for t in range(TASKS):
                    at = pl.ds(pl.multiple_of((step * TASKS + t) * BLK, BLK), BLK)
                    att[span, head, at, :] = done[t]
                return inner

            lax.fori_loop(0, query_blocks // TASKS, tasks, 0)

            def send_out(k, inner):
                out_copy(span, head, k, lax.rem(me + k, n), me).start()
                return inner

            lax.fori_loop(0, n, send_out, 0)
            return carry

        lax.fori_loop(0, heads, one_head, 0)

    for span in range(spans):
        for item in range(items):

            def sent(k, carry):
                in_copy(span, item, k, lax.rem(me + k, n), me).wait_send()
                return carry

            lax.fori_loop(1, n, sent, 0)

        def head_done(head, carry):
            def both(k, inner):
                out_copy(span, head, k, lax.rem(me + k, n), me).wait_send()
                out_copy(
                    span, head, k, lax.rem(me + k, n), lax.rem(me + n - k, n)
                ).wait_recv()
                return inner

            return lax.fori_loop(0, n, both, carry)

        lax.fori_loop(0, heads, head_done, 0)


def on_device(
    queries, keys_new, values_new, key_cache, value_cache, block_lists, block_counts, visible_blocks
):
    n = lax.axis_size("seq")
    sections = lax.axis_size("section")
    spans, rows = queries.shape[1], queries.shape[2]
    heads, context = key_cache.shape[1], key_cache.shape[2]
    kv_dev = max(1, heads // GROUP)
    span_len = rows * n
    items = 2 * kv_dev + heads
    slots = block_lists.shape[4]
    smem = pl.BlockSpec(memory_space=pltpu.MemorySpace.SMEM)
    vmem = pl.BlockSpec(memory_space=pltpu.MemorySpace.VMEM)
    anywhere = pl.BlockSpec(memory_space=pl.ANY)
    usable = (jnp.arange(slots) < block_counts[0][..., None]) & (
        block_lists[0] < visible_blocks[None, :, None, None]
    )
    biases = jnp.where(usable, 0.0, -jnp.inf).astype(jnp.float32)
    biases = jnp.repeat(biases, BLK, axis=3).reshape(-1, slots // CHUNK, CHUNK * BLK)
    dma = pltpu.SemaphoreType.DMA
    return pl.pallas_call(
        functools.partial(fused, n, sections),
        out_shape=jax.ShapeDtypeStruct(queries.shape, queries.dtype),
        in_specs=[smem, vmem] + [anywhere] * 5,
        out_specs=anywhere,
        scratch_shapes=[
            pltpu.VMEM((spans, heads, span_len, DH), jnp.bfloat16),
            pltpu.VMEM((spans, kv_dev, span_len, DH), jnp.bfloat16),
            pltpu.VMEM((spans, kv_dev, span_len, DH), jnp.bfloat16),
            pltpu.VMEM((heads, context // BLK, BLK, DH), jnp.bfloat16),
            pltpu.VMEM((heads, context // BLK, BLK, DH), jnp.bfloat16),
            pltpu.VMEM((spans, heads, span_len, DH), jnp.bfloat16),
            pltpu.VMEM((span_len, DH), jnp.float32),
            pltpu.VMEM((span_len, DH), jnp.float32),
            pltpu.VMEM((span_len, DH), jnp.float32),
            dma((spans, items, n)),
            dma((spans, items, n)),
            dma((spans, items)),
            dma((2, heads)),
            dma((spans, heads, n)),
            dma((spans, heads, n)),
        ],
        compiler_params=pltpu.CompilerParams(
            collective_id=0, has_side_effects=True, vmem_limit_bytes=60 << 20
        ),
    )(
        block_lists.reshape(-1, slots),
        biases,
        queries,
        keys_new,
        values_new,
        key_cache.reshape(1, heads, context // BLK, BLK, DH),
        value_cache.reshape(1, heads, context // BLK, BLK, DH),
    )


def solution(mesh):
    return jax.shard_map(
        on_device,
        mesh=mesh,
        in_specs=(
            P("section", None, "seq", None),
            P("section", None, "seq", None),
            P("section", None, "seq", None),
            P("section", "seq", None, None),
            P("section", "seq", None, None),
            P("section", "seq", None, None, None),
            P("section", "seq", None, None),
            P(),
        ),
        out_specs=P("section", None, "seq", None),
        check_vma=False,
    )
```

```python
import functools
import math

import jax
import jax.numpy as jnp
from jax import lax
from jax.experimental import pallas as pl
from jax.experimental.pallas import tpu as pltpu
from jax.sharding import PartitionSpec as P

HEADS = 32
KVH = 8
DH = 128
BLK = 64
GROUP = HEADS // KVH
ROW_TILE = 256
CHUNK = 4
TASKS = 4


def mesh_copy(src, dst, send_sem, recv_sem, section, seq):
    return pltpu.make_async_remote_copy(
        src_ref=src,
        dst_ref=dst,
        send_sem=send_sem,
        recv_sem=recv_sem,
        device_id=(section, seq),
        device_id_type=pl.DeviceIdType.MESH,
    )


def scores_of(query, keys):
    return lax.dot_general(
        query, keys, (((1,), (1,)), ((), ())), preferred_element_type=jnp.float32
    )


def fused(
    n,
    sections,
    lists,
    biases,
    queries,
    keys_new,
    values_new,
    key_cache,
    value_cache,
    out,
    qbuf,
    kbuf,
    vbuf,
    ckeys,
    cvalues,
    att,
    own_max,
    own_sum,
    own_out,
    in_send,
    in_recv,
    in_local,
    cache_sem,
    out_send,
    out_recv,
):
    spans, heads, span_len = qbuf.shape[0], qbuf.shape[1], qbuf.shape[2]
    kv_dev = kbuf.shape[1]
    rows = queries.shape[2]
    slots = lists.shape[1]
    query_blocks = span_len // BLK
    items = 2 * kv_dev + heads
    weight_scale = math.log2(math.e) / math.sqrt(DH)
    section = lax.axis_index("section")
    me = lax.axis_index("seq")
    above = lax.rem(section + 1, sections)
    below = lax.rem(section + sections - 1, sections)

    for head in range(heads):
        pltpu.make_async_copy(key_cache.at[0, head], ckeys.at[head], cache_sem.at[0, head]).start()
        pltpu.make_async_copy(
            value_cache.at[0, head], cvalues.at[head], cache_sem.at[1, head]
        ).start()

    def source(span, item, seq):
        if isinstance(item, int) and item < 2 * kv_dev:
            array = keys_new if item < kv_dev else values_new
            column = lax.div(seq * heads, GROUP) * DH + (item % kv_dev) * DH
        else:
            array = queries
            column = (seq * heads + item - 2 * kv_dev) * DH
        return array.at[0, span, :, pl.ds(pl.multiple_of(column, DH), DH)]

    def landing(span, item, seq):
        where = pl.ds(pl.multiple_of(seq * rows, rows), rows)
        if isinstance(item, int) and item < kv_dev:
            return kbuf.at[span, item, where, :]
        if isinstance(item, int) and item < 2 * kv_dev:
            return vbuf.at[span, item - kv_dev, where, :]
        return qbuf.at[span, item - 2 * kv_dev, where, :]

    def own_copy(span, item):
        return pltpu.make_async_copy(
            source(span, item, me), landing(span, item, me), in_local.at[span, item]
        )

    for span in range(spans):
        for item in range(items):
            own_copy(span, item).start()

    barrier = pltpu.get_barrier_semaphore()

    def greet(k, carry):
        @pl.when(k > 0)
        def _():
            pl.semaphore_signal(
                barrier,
                inc=1,
                device_id=(section, lax.rem(me + k, n)),
                device_id_type=pl.DeviceIdType.MESH,
            )

        for there in (above, below):
            pl.semaphore_signal(
                barrier,
                inc=1,
                device_id=(there, lax.rem(me + k, n)),
                device_id_type=pl.DeviceIdType.MESH,
            )
        return carry

    lax.fori_loop(0, n, greet, 0)
    pl.semaphore_wait(barrier, 3 * n - 1)

    def in_copy(span, item, k, seq_to, seq_from):
        return mesh_copy(
            source(span, item, seq_to),
            landing(span, item, seq_from),
            in_send.at[span, item, k],
            in_recv.at[span, item, k],
            section,
            seq_to,
        )

    for span in range(spans):
        for item in range(items):

            def send_in(k, carry):
                in_copy(span, item, k, lax.rem(me + k, n), me).start()
                return carry

            lax.fori_loop(1, n, send_in, 0)

    def await_in(span, item):
        own_copy(span, item).wait()

        def one(k, carry):
            in_copy(
                span, item, k, lax.rem(me + k, n), lax.rem(me + n - k, n)
            ).wait_recv()
            return carry

        lax.fori_loop(1, n, one, 0)

    def out_copy(span, head, k, seq_to, seq_from):
        column = pl.multiple_of((seq_from * heads + head) * DH, DH)
        return mesh_copy(
            att.at[span, head, pl.ds(pl.multiple_of(seq_to * rows, rows), rows), :],
            out.at[0, span, :, pl.ds(column, DH)],
            out_send.at[span, head, k],
            out_recv.at[span, head, k],
            above,
            seq_to,
        )

    row_at = lax.broadcasted_iota(jnp.int32, (ROW_TILE, ROW_TILE), 0)
    key_at = lax.broadcasted_iota(jnp.int32, (ROW_TILE, ROW_TILE), 1)

    def weigh(scores, top):
        return jnp.exp2((scores - top) * weight_scale)

    def own_part(span, head, kv, tile):
        start = tile * ROW_TILE
        query = qbuf[span, head, start : start + ROW_TILE, :]
        parts = []
        for piece in range(tile + 1):
            keys = kbuf[span, kv, piece * ROW_TILE : (piece + 1) * ROW_TILE, :]
            scores = scores_of(query, keys)
            if piece == tile:
                scores = jnp.where(row_at >= key_at, scores, -jnp.inf)
            parts.append(scores)
        top = jnp.max(functools.reduce(jnp.maximum, parts), axis=1, keepdims=True)
        summed, mixed = None, None
        for piece, scores in enumerate(parts):
            weights = weigh(scores, top)
            values = vbuf[span, kv, piece * ROW_TILE : (piece + 1) * ROW_TILE, :]
            product = jnp.dot(
                weights.astype(jnp.bfloat16), values, preferred_element_type=jnp.float32
            )
            summed = weights if summed is None else summed + weights
            mixed = product if mixed is None else mixed + product
        total = jnp.sum(summed, axis=1, keepdims=True)
        own_max[start : start + ROW_TILE, :] = jnp.broadcast_to(top, (ROW_TILE, DH))
        own_sum[start : start + ROW_TILE, :] = jnp.broadcast_to(total, (ROW_TILE, DH))
        own_out[start : start + ROW_TILE, :] = mixed

    def cache_part(span, head, block):
        listed = (head * spans + span) * query_blocks + block
        at = pl.ds(pl.multiple_of(block * BLK, BLK), BLK)
        query = qbuf[span, head, at, :]
        chosen = [lists[listed, i] for i in range(slots)]
        bias = biases[listed]
        parts = []
        for first in range(0, slots, CHUNK):
            keys = jnp.concatenate(
                [
                    ckeys[head, chosen[i]]
                    for i in range(first, first + CHUNK)
                ],
                axis=0,
            )
            scores = scores_of(query, keys)
            parts.append(scores + bias[first // CHUNK : first // CHUNK + 1, :])
        before = own_max[at, :][:, :1]
        top = jnp.max(functools.reduce(jnp.maximum, parts), axis=1, keepdims=True)
        top = jnp.maximum(top, before)
        summed, mixed = None, None
        for step, scores in enumerate(parts):
            weights = weigh(scores, top)
            values = jnp.concatenate(
                [
                    cvalues[head, chosen[i]]
                    for i in range(step * CHUNK, (step + 1) * CHUNK)
                ],
                axis=0,
            )
            product = jnp.dot(
                weights.astype(jnp.bfloat16), values, preferred_element_type=jnp.float32
            )
            summed = weights if summed is None else summed + weights
            mixed = product if mixed is None else mixed + product
        fade = weigh(before, top)
        total = jnp.sum(summed, axis=1, keepdims=True) + own_sum[at, :][:, :1] * fade
        return ((mixed + own_out[at, :] * fade) / total).astype(jnp.bfloat16)

    for head in range(heads):
        pltpu.make_async_copy(key_cache.at[0, head], ckeys.at[head], cache_sem.at[0, head]).wait()
        pltpu.make_async_copy(
            value_cache.at[0, head], cvalues.at[head], cache_sem.at[1, head]
        ).wait()

    for span in range(spans):
        for item in range(2 * kv_dev):
            await_in(span, item)

        def one_head(head, carry):
            kv = lax.div(head, GROUP)
            await_in(span, 2 * kv_dev + head)
            for tile in range(span_len // ROW_TILE):
                own_part(span, head, kv, tile)

            def tasks(step, inner):
                done = [cache_part(span, head, step * TASKS + t) for t in range(TASKS)]
                for t in range(TASKS):
                    at = pl.ds(pl.multiple_of((step * TASKS + t) * BLK, BLK), BLK)
                    att[span, head, at, :] = done[t]
                return inner

            lax.fori_loop(0, query_blocks // TASKS, tasks, 0)

            def send_out(k, inner):
                out_copy(span, head, k, lax.rem(me + k, n), me).start()
                return inner

            lax.fori_loop(0, n, send_out, 0)
            return carry

        lax.fori_loop(0, heads, one_head, 0)

    for span in range(spans):
        for item in range(items):

            def sent(k, carry):
                in_copy(span, item, k, lax.rem(me + k, n), me).wait_send()
                return carry

            lax.fori_loop(1, n, sent, 0)

        def head_done(head, carry):
            def both(k, inner):
                out_copy(span, head, k, lax.rem(me + k, n), me).wait_send()
                out_copy(
                    span, head, k, lax.rem(me + k, n), lax.rem(me + n - k, n)
                ).wait_recv()
                return inner

            return lax.fori_loop(0, n, both, carry)

        lax.fori_loop(0, heads, head_done, 0)


def on_device(
    queries, keys_new, values_new, key_cache, value_cache, block_lists, block_counts, visible_blocks
):
    n = lax.axis_size("seq")
    sections = lax.axis_size("section")
    spans, rows = queries.shape[1], queries.shape[2]
    heads, context = key_cache.shape[1], key_cache.shape[2]
    kv_dev = max(1, heads // GROUP)
    span_len = rows * n
    items = 2 * kv_dev + heads
    slots = block_lists.shape[4]
    smem = pl.BlockSpec(memory_space=pltpu.MemorySpace.SMEM)
    vmem = pl.BlockSpec(memory_space=pltpu.MemorySpace.VMEM)
    anywhere = pl.BlockSpec(memory_space=pl.ANY)
    usable = (jnp.arange(slots) < block_counts[0][..., None]) & (
        block_lists[0] < visible_blocks[None, :, None, None]
    )
    biases = jnp.where(usable, 0.0, -jnp.inf).astype(jnp.float32)
    biases = jnp.repeat(biases, BLK, axis=3).reshape(-1, slots // CHUNK, CHUNK * BLK)
    dma = pltpu.SemaphoreType.DMA
    return pl.pallas_call(
        functools.partial(fused, n, sections),
        out_shape=jax.ShapeDtypeStruct(queries.shape, queries.dtype),
        in_specs=[smem, vmem] + [anywhere] * 5,
        out_specs=anywhere,
        scratch_shapes=[
            pltpu.VMEM((spans, heads, span_len, DH), jnp.bfloat16),
            pltpu.VMEM((spans, kv_dev, span_len, DH), jnp.bfloat16),
            pltpu.VMEM((spans, kv_dev, span_len, DH), jnp.bfloat16),
            pltpu.VMEM((heads, context // BLK, BLK, DH), jnp.bfloat16),
            pltpu.VMEM((heads, context // BLK, BLK, DH), jnp.bfloat16),
            pltpu.VMEM((spans, heads, span_len, DH), jnp.bfloat16),
            pltpu.VMEM((span_len, DH), jnp.float32),
            pltpu.VMEM((span_len, DH), jnp.float32),
            pltpu.VMEM((span_len, DH), jnp.float32),
            dma((spans, items, n)),
            dma((spans, items, n)),
            dma((spans, items)),
            dma((2, heads)),
            dma((spans, heads, n)),
            dma((spans, heads, n)),
        ],
        compiler_params=pltpu.CompilerParams(
            collective_id=0, has_side_effects=True, vmem_limit_bytes=60 << 20
        ),
    )(
        block_lists.reshape(-1, slots),
        biases,
        queries,
        keys_new,
        values_new,
        key_cache.reshape(1, heads, context // BLK, BLK, DH),
        value_cache.reshape(1, heads, context // BLK, BLK, DH),
    )


def solution(mesh):
    return jax.shard_map(
        on_device,
        mesh=mesh,
        in_specs=(
            P("section", None, "seq", None),
            P("section", None, "seq", None),
            P("section", None, "seq", None),
            P("section", "seq", None, None),
            P("section", "seq", None, None),
            P("section", "seq", None, None, None),
            P("section", "seq", None, None),
            P(),
        ),
        out_specs=P("section", None, "seq", None),
        check_vma=False,
    )
```
